32 devices in a mesh: seq: 8 (over z, core), head: 4 (over y, x).
Axes of the slice: x: 2, y: 2, z: 4, core: 2. Of those that a mesh axis runs over, the one named last changes fastest.
Arguments:
- attn_query: bfloat16 [16384, 2560], P('seq', 'head'), may hold values from -45 to 45
- attn_key: bfloat16 [16384, 2560], P('seq', 'head'), may hold values from -15 to 15
- attn_value: bfloat16 [16384, 2560], P('seq', 'head'), may hold values from -6 to 6
- fast_query: bfloat16 [16384, 2560], P('seq', 'head'), may hold values from -6 to 6
- fast_key: bfloat16 [16384, 2560], P('seq', 'head'), may hold values from -6 to 6
- fast_value: bfloat16 [16384, 2560], P('seq', 'head'), may hold values from -6 to 6
- rates: float32 [16384, 4], P('seq', 'head'), may hold values from 0.00022097086 to 0.0022097088
- fast_weights: float32 [4, 640, 3, 640], P('head'), may hold values from -0.25 to 0.25
- gain: float32 [4, 640], P('head'), may hold values from 0.5 to 1.5
Outputs:
- mixed: bfloat16 [16384, 2560], P('seq', 'head')
- final_weights: float32 [4, 640, 3, 640], P('head', 'seq')
The draws below stay inside these ranges and needn't reach their ends.
All inputs are finite; a program needn't handle non-finite values.
Results may differ from the reference program's by a relative error of at most 0.013.
Values may be sent and summed in bfloat16 or wider, within the bound.
A program may use at most 192 MiB of HBM per device.

```python
import math
import jax
import jax.numpy as jnp
from jax import lax

DH = 640
FH = 640
AH = 128
WINDOW = 512
HEADS = 4
ATT_HEADS = 20
TOKENS = 16384


def attention_pair(seed_key):
    grid_shape = (TOKENS, ATT_HEADS * AH)
    base_key = jnp.clip(jax.random.normal(jax.random.fold_in(seed_key, 101), grid_shape, jnp.float32), -5.0, 5.0)
    base_query = jnp.clip(jax.random.normal(jax.random.fold_in(seed_key, 202), grid_shape, jnp.float32), -5.0, 5.0)
    return (base_query, base_key)


def draw_attn_query(key, part):
    return attention_pair(key)[0].astype(jnp.bfloat16)


def draw_attn_key(key, part):
    return attention_pair(key)[1].astype(jnp.bfloat16)


def level_of(key, dims, split, smallest, high):
    def one(axis_at, parts):
        steps = jax.random.uniform(jax.random.fold_in(jax.random.fold_in(key, 6), axis_at), (parts,), jnp.float32, smallest / len(split), high / len(split))
        return jnp.repeat(jnp.exp(steps), dims[axis_at] // parts).reshape((-1,) + (1,) * (len(dims) - axis_at - 1))

    level = one(*split[0])
    for cut in split[1:]:
        level = level * one(*cut)
    return level


def normal_values(own_key, dims, scale, reach, cuts=(), held_as=jnp.bfloat16):
    drawn = jax.random.normal(own_key, dims, jnp.float32) * scale
    if len(cuts) > 0:
        drawn = level_of(own_key, dims, cuts, -0.22, 0.18) * drawn
    return jnp.clip(drawn, min=-reach, max=reach).astype(held_as)


def setup_inputs(seed: int = 0) -> dict:
    arg_keys = jax.random.split(jax.random.key(seed), 10)
    attn_query = draw_attn_query(jax.random.fold_in(arg_keys[9], 71), 0)
    attn_key = draw_attn_key(jax.random.fold_in(arg_keys[9], 71), 0)
    attn_value = normal_values(arg_keys[2], (TOKENS, ATT_HEADS * AH), 1.0, 6.0, ((0, 8), (1, 4)))
    fast_query = normal_values(arg_keys[3], (TOKENS, HEADS * DH), 1.0, 6.0, ((0, 8), (1, 4)))
    fast_key = normal_values(arg_keys[4], (TOKENS, HEADS * DH), 1.0, 6.0, ((0, 8), (1, 4)))
    fast_value = normal_values(arg_keys[5], (TOKENS, HEADS * DH), 1.0, 6.0, ((0, 8), (1, 4)))
    rates = jnp.clip(jnp.exp(math.log(0.0022097088) - 2.3025852 * jax.random.uniform(arg_keys[6], (TOKENS, HEADS), jnp.float32) ** level_of(arg_keys[6], (TOKENS, HEADS), ((0, 8), (1, 4)), -0.2, 0.2)), 0.00022097086, 0.0022097088)
    fast_weights = normal_values(arg_keys[7], (HEADS, FH, 3, DH), DH ** -0.5, 0.25, ((0, 4),), jnp.float32)
    gain = jnp.clip(1.0 + 0.1 * jax.random.normal(arg_keys[8], (HEADS, DH), jnp.float32), 0.5, 1.5)
    return dict(attn_query=attn_query, attn_key=attn_key, attn_value=attn_value, fast_query=fast_query, fast_key=fast_key, fast_value=fast_value, rates=rates, fast_weights=fast_weights, gain=gain)


EPSILON = 1e-06

def window_attention(queries, key_rows, value_rows):
    total_rows, columns = queries.shape
    head_count = columns // AH
    tile_rows = min(total_rows, 512)
    zero_rows = jnp.zeros((WINDOW, columns), queries.dtype)
    padded_keys = jnp.concatenate([zero_rows, key_rows], 0)
    padded_values = jnp.concatenate([zero_rows, value_rows], 0)

    def one_tile(tile_index):
        tile_start = tile_index * tile_rows
        query_tile = lax.dynamic_slice_in_dim(queries, tile_start, tile_rows, 0).astype(jnp.float32).reshape(tile_rows, head_count, AH)
        key_tile = lax.dynamic_slice_in_dim(padded_keys, tile_start, tile_rows + WINDOW, 0).astype(jnp.float32).reshape(tile_rows + WINDOW, head_count, AH)
        value_tile = lax.dynamic_slice_in_dim(padded_values, tile_start, tile_rows + WINDOW, 0).astype(jnp.float32).reshape(tile_rows + WINDOW, head_count, AH)
        scores = jnp.einsum('qhd,khd->hqk', query_tile, key_tile) * (1.0 / math.sqrt(AH))
        query_pos = tile_start + jnp.arange(tile_rows, dtype=jnp.int32)
        key_pos = tile_start - WINDOW + jnp.arange(tile_rows + WINDOW, dtype=jnp.int32)
        distance = query_pos[:, None] - key_pos[None, :]
        allowed = (distance >= 0) & (distance < WINDOW) & (key_pos[None, :] >= 0)
        scores = jnp.where(allowed[None], scores, -1e+30)
        row_max = lax.optimization_barrier(jnp.max(scores, axis=-1, keepdims=True))
        weights = jnp.exp(scores - row_max)
        row_total = lax.optimization_barrier(jnp.sum(weights, axis=-1, keepdims=True))
        probabilities = (weights / row_total).astype(jnp.bfloat16)
        result = jnp.einsum('hqk,khd->qhd', probabilities.astype(jnp.float32), value_tile)
        return result.reshape(tile_rows, columns)
    tiles = lax.map(one_tile, jnp.arange(total_rows // tile_rows, dtype=jnp.int32))
    return tiles.reshape(total_rows, columns)

def block_gradient(weights, key_rows, value_rows, rate_rows):
    gate_pre = jnp.dot(key_rows, weights[:, 0, :].T, preferred_element_type=jnp.float32)
    up_pre = jnp.dot(key_rows, weights[:, 1, :].T, preferred_element_type=jnp.float32)
    active = jax.nn.silu(gate_pre)
    hidden = (active * up_pre).astype(jnp.bfloat16)
    signal = (rate_rows * value_rows.astype(jnp.float32)).astype(jnp.bfloat16)
    back_grad = jnp.dot(signal, weights[:, 2, :].T, preferred_element_type=jnp.float32)
    sigmoid_gate = jax.nn.sigmoid(gate_pre)
    up_grad = (back_grad * active).astype(jnp.bfloat16)
    gate_grad = (back_grad * up_pre * sigmoid_gate * (1.0 + gate_pre * (1.0 - sigmoid_gate))).astype(jnp.bfloat16)
    gate_term = jnp.dot(gate_grad.T, key_rows, preferred_element_type=jnp.float32)
    up_term = jnp.dot(up_grad.T, key_rows, preferred_element_type=jnp.float32)
    down_term = jnp.dot(hidden.T, signal, preferred_element_type=jnp.float32)
    return jnp.stack([gate_term, up_term, down_term], axis=1)

def renormalize(previous, gradient):
    moved = previous + gradient
    norm_ratio = jnp.sqrt(lax.optimization_barrier(jnp.mean(previous * previous, axis=-1, keepdims=True)) + EPSILON) / jnp.sqrt(lax.optimization_barrier(jnp.mean(moved * moved, axis=-1, keepdims=True)) + EPSILON)
    return moved * norm_ratio

def fast_apply(weights, query_rows, gain_row):
    gate_pre = jnp.dot(query_rows, weights[:, 0, :].T, preferred_element_type=jnp.float32)
    up_pre = jnp.dot(query_rows, weights[:, 1, :].T, preferred_element_type=jnp.float32)
    hidden = (jax.nn.silu(gate_pre) * up_pre).astype(jnp.bfloat16)
    output = jnp.dot(hidden, weights[:, 2, :], preferred_element_type=jnp.float32)
    inverse_rms = lax.rsqrt(lax.optimization_barrier(jnp.mean(output * output, axis=-1, keepdims=True)) + EPSILON)
    return output * inverse_rms * gain_row

def reference(attn_query, attn_key, attn_value, fast_query, fast_key, fast_value, rates, fast_weights, gain):
    attended = window_attention(attn_query, attn_key, attn_value)
    half_rows = TOKENS // 2
    pieces = []
    finals = []
    for head_index in range(HEADS):
        low = head_index * DH
        head_queries = fast_query[:, low:low + DH]
        head_keys = fast_key[:, low:low + DH]
        head_values = fast_value[:, low:low + DH]
        head_rates = rates[:, head_index:head_index + 1]
        initial = fast_weights[head_index]
        first_cast = initial.astype(jnp.bfloat16)
        first_gradient = block_gradient(first_cast, head_keys[:half_rows], head_values[:half_rows], head_rates[:half_rows])
        middle = renormalize(initial, first_gradient)
        middle_cast = middle.astype(jnp.bfloat16)
        second_gradient = block_gradient(middle_cast, head_keys[half_rows:], head_values[half_rows:], head_rates[half_rows:])
        finals.append(renormalize(middle, second_gradient))
        early_out = fast_apply(first_cast, head_queries[:half_rows], gain[head_index])
        later_out = fast_apply(middle_cast, head_queries[half_rows:], gain[head_index])
        pieces.append(jnp.concatenate([early_out, later_out], 0))
    mixed = (attended + jnp.concatenate(pieces, 1)).astype(jnp.bfloat16)
    return (mixed, jnp.stack(finals))
```

```python
import functools
import math

import jax
import jax.numpy as jnp
from jax import lax
from jax.experimental import pallas as pl
from jax.experimental.pallas import tpu as pltpu
from jax.sharding import PartitionSpec as P

AH = 128
WINDOW = 512
EPSILON = 1e-06
NEG = -1e30
NT = (((1,), (1,)), ((), ()))
NN = (((1,), (0,)), ((), ()))
LIMIT = 60 * 1024 * 1024


def mm(a, b, dims):
    return lax.dot_general(a, b, dims, preferred_element_type=jnp.float32)


def sigmoid(v):
    return 0.5 * jnp.tanh(0.5 * v) + 0.5


def attend(q, keys, values, biases):
    rows = q.shape[0]
    factor = math.log2(math.e) / math.sqrt(AH)
    old, mid, new = (mm(q, k, NT) for k in keys)
    if biases[0] is not None:
        old = old + biases[0]
    if biases[1] is not None:
        mid = mid + biases[1]
    row = lax.broadcasted_iota(jnp.int32, (rows, rows), 0)
    col = lax.broadcasted_iota(jnp.int32, (rows, rows), 1)
    causal = col <= row
    edge = jnp.where(causal, new, old)
    top = jnp.maximum(jnp.max(edge, -1, keepdims=True), jnp.max(mid, -1, keepdims=True))
    edge = jnp.exp2((edge - top) * factor)
    mid = jnp.exp2((mid - top) * factor)
    total = jnp.sum(edge, -1, keepdims=True) + jnp.sum(mid, -1, keepdims=True)
    p_new = jnp.where(causal, edge, 0.0).astype(jnp.bfloat16)
    p_old = jnp.where(causal, 0.0, edge).astype(jnp.bfloat16)
    out = mm(p_new, values[2], NN) + mm(p_old, values[0], NN)
    out = out + mm(mid.astype(jnp.bfloat16), values[1], NN)
    return out * (1.0 / total)


def attention_kernel(q_ref, k_ref, v_ref, hk_ref, hv_ref, o_ref):
    tile = WINDOW // 2
    bias = jnp.where(lax.axis_index("seq") == 0, jnp.float32(NEG), jnp.float32(0.0))

    def block(ref, halo, at):
        if at < 0:
            return halo[(at + 2) * tile : (at + 3) * tile, :]
        return ref[at * tile : (at + 1) * tile, :]

    for t in range(q_ref.shape[0] // tile):
        keys = [block(k_ref, hk_ref, t - 2 + i) for i in range(3)]
        values = [block(v_ref, hv_ref, t - 2 + i) for i in range(3)]
        biases = [bias if t - 2 + i < 0 else None for i in range(2)]
        o_ref[t * tile : (t + 1) * tile, :] = attend(
            q_ref[t * tile : (t + 1) * tile, :], keys, values, biases
        )


def attention(q, k, v, hk, hv):
    rows, columns = q.shape
    part = pl.BlockSpec((rows, AH), lambda h: (0, h))
    halo = pl.BlockSpec((WINDOW, AH), lambda h: (0, h))
    return pl.pallas_call(
        attention_kernel,
        grid=(columns // AH,),
        out_shape=jax.ShapeDtypeStruct((rows, columns), jnp.float32),
        in_specs=[part, part, part, halo, halo],
        out_specs=part,
        compiler_params=pltpu.CompilerParams(vmem_limit_bytes=LIMIT),
        cost_estimate=pl.CostEstimate(
            flops=4 * rows * columns * WINDOW * 4, bytes_accessed=10 * rows * columns, transcendentals=0
        ),
    )(q, k, v, hk, hv)


def grad_parts(w_ref, x, val, rate):
    signal = (rate * val.astype(jnp.float32)).astype(jnp.bfloat16)
    gate = mm(w_ref[0], x, NT)
    up = mm(w_ref[1], x, NT)
    back = mm(w_ref[2], signal, NT)
    s = sigmoid(gate)
    active = gate * s
    hidden = (active * up).astype(jnp.bfloat16)
    up_grad = (back * active).astype(jnp.bfloat16)
    gate_grad = (back * up * (s * (1.0 + gate * (1.0 - s)))).astype(jnp.bfloat16)
    return mm(gate_grad, x, NN), mm(up_grad, x, NN), mm(hidden, signal, NN)


def gradient_kernel(block, half, w_ref, x_ref, val_ref, rate_ref, o_ref, acc):
    active = lax.axis_index("seq") // half == block
    step = pl.program_id(0)
    last = pl.num_programs(0) - 1

    @pl.when(active)
    def _():
        parts = grad_parts(w_ref, x_ref[...], val_ref[...], rate_ref[...])
        for i in range(3):
            @pl.when(step == 0)
            def _():
                acc[i] = parts[i]

            @pl.when(step > 0)
            def _():
                acc[i] += parts[i]

            @pl.when(step == last)
            def _():
                o_ref[i] = acc[i].astype(o_ref.dtype)

    @pl.when(jnp.logical_not(active) & (step == last))
    def _():
        o_ref[...] = jnp.zeros_like(o_ref)


def gradient(block, half, w, x, val, rate):
    rows, d = x.shape
    f = w.shape[1]
    m = min(rows, 512)
    return pl.pallas_call(
        functools.partial(gradient_kernel, block, half),
        grid=(rows // m,),
        out_shape=jax.ShapeDtypeStruct((3, f, d), jnp.bfloat16),
        in_specs=[
            pl.BlockSpec((3, f, d), lambda i: (0, 0, 0)),
            pl.BlockSpec((m, d), lambda i: (i, 0)),
            pl.BlockSpec((m, d), lambda i: (i, 0)),
            pl.BlockSpec((m, 1), lambda i: (i, 0)),
        ],
        out_specs=pl.BlockSpec((3, f, d), lambda i: (0, 0, 0)),
        scratch_shapes=[pltpu.VMEM((3, f, d), jnp.float32)],
        compiler_params=pltpu.CompilerParams(vmem_limit_bytes=LIMIT),
    )(w, x, val, rate)


def apply_tile(w_ref, x, gain):
    gate = mm(x, w_ref[0], NT)
    up = mm(x, w_ref[1], NT)
    hidden = (gate * sigmoid(gate) * up).astype(jnp.bfloat16)
    out = mm(hidden, w_ref[2], NN)
    inverse = lax.rsqrt(jnp.mean(out * out, axis=-1, keepdims=True) + EPSILON)
    return out * inverse * gain


def apply_kernel(w_ref, x_ref, gain_ref, att_ref, o_ref):
    o_ref[...] = (att_ref[...] + apply_tile(w_ref, x_ref[...], gain_ref[...])).astype(o_ref.dtype)


def apply(w, x, gain, attended):
    rows, d = x.shape
    f = w.shape[1]
    m = min(rows, 512)
    tile = pl.BlockSpec((m, d), lambda i: (i, 0))
    return pl.pallas_call(
        apply_kernel,
        grid=(rows // m,),
        out_shape=jax.ShapeDtypeStruct((rows, d), jnp.bfloat16),
        in_specs=[
            pl.BlockSpec((3, f, d), lambda i: (0, 0, 0)),
            tile,
            pl.BlockSpec((1, d), lambda i: (0, 0)),
            tile,
        ],
        out_specs=tile,
        compiler_params=pltpu.CompilerParams(vmem_limit_bytes=LIMIT),
        cost_estimate=pl.CostEstimate(flops=12 * rows * d * f, bytes_accessed=10 * rows * d, transcendentals=0),
    )(w, x, gain, attended)


def renormalize(previous, grad):
    moved = previous + grad
    return moved * (
        jnp.sqrt(jnp.mean(previous * previous, axis=-1, keepdims=True) + EPSILON)
        / jnp.sqrt(jnp.mean(moved * moved, axis=-1, keepdims=True) + EPSILON)
    )


def shards(
    attn_query, attn_key, attn_value, fast_query, fast_key, fast_value, rates, fast_weights, gain
):
    count = lax.axis_size("seq")
    seq = lax.axis_index("seq")
    half = count // 2
    pairs = [(i, i + 1) for i in range(count - 1)]
    halo_k, halo_v = lax.ppermute((attn_key[-WINDOW:], attn_value[-WINDOW:]), "seq", pairs)
    initial = jnp.swapaxes(fast_weights[0], 0, 1)
    first_cast = initial.astype(jnp.bfloat16)
    share = initial.shape[1] // count

    first = gradient(0, half, first_cast, fast_key, fast_value, rates)
    first_part = lax.psum_scatter(first, "seq", scatter_dimension=1, tiled=True)
    attended = attention(attn_query, attn_key, attn_value, halo_k, halo_v)
    middle_rows = renormalize(
        lax.dynamic_slice_in_dim(initial, seq * share, share, 1), first_part.astype(jnp.float32)
    )
    middle_cast = lax.all_gather(middle_rows.astype(jnp.bfloat16), "seq", axis=1, tiled=True)
    second = gradient(1, half, middle_cast, fast_key, fast_value, rates)
    second_part = lax.psum_scatter(second, "seq", scatter_dimension=1, tiled=True)
    mixed = apply(jnp.where(seq < half, first_cast, middle_cast), fast_query, gain, attended)
    final_rows = renormalize(middle_rows, second_part.astype(jnp.float32))
    return (mixed, jnp.swapaxes(final_rows, 0, 1)[None])


def solution(mesh):
    tokens = P("seq", "head")
    in_specs = (tokens,) * 7 + (P("head", None, None, None), P("head", None))
    out_specs = (tokens, P("head", "seq", None, None))
    return jax.shard_map(shards, mesh=mesh, in_specs=in_specs, out_specs=out_specs, check_vma=False)
```

```python
import functools
import math

import jax
import jax.numpy as jnp
from jax import lax
from jax.experimental import pallas as pl
from jax.experimental.pallas import tpu as pltpu
from jax.sharding import PartitionSpec as P

AH = 128
WINDOW = 512
EPSILON = 1e-06
NEG = -1e30
NT = (((1,), (1,)), ((), ()))
NN = (((1,), (0,)), ((), ()))
LIMIT = 60 * 1024 * 1024
SLICES = 4


def mm(a, b, dims):
    return lax.dot_general(a, b, dims, preferred_element_type=jnp.float32)


def sigmoid(v):
    return 0.5 * jnp.tanh(0.5 * v) + 0.5


def attend(q, keys, values, biases):
    rows = q.shape[0]
    factor = math.log2(math.e) / math.sqrt(AH)
    old, mid, new = (mm(q, k, NT) for k in keys)
    if biases[0] is not None:
        old = old + biases[0]
    if biases[1] is not None:
        mid = mid + biases[1]
    row = lax.broadcasted_iota(jnp.int32, (rows, rows), 0)
    col = lax.broadcasted_iota(jnp.int32, (rows, rows), 1)
    causal = col <= row
    edge = jnp.where(causal, new, old)
    top = jnp.maximum(jnp.max(edge, -1, keepdims=True), jnp.max(mid, -1, keepdims=True))
    edge = jnp.exp2((edge - top) * factor)
    mid = jnp.exp2((mid - top) * factor)
    total = jnp.sum(edge, -1, keepdims=True) + jnp.sum(mid, -1, keepdims=True)
    p_new = jnp.where(causal, edge, 0.0).astype(jnp.bfloat16)
    p_old = jnp.where(causal, 0.0, edge).astype(jnp.bfloat16)
    out = mm(p_new, values[2], NN) + mm(p_old, values[0], NN)
    out = out + mm(mid.astype(jnp.bfloat16), values[1], NN)
    return out * (1.0 / total)


def apply_tile(w_ref, x, gain):
    gate = mm(x, w_ref[0], NT)
    up = mm(x, w_ref[1], NT)
    hidden = (gate * sigmoid(gate) * up).astype(jnp.bfloat16)
    out = mm(hidden, w_ref[2], NN)
    inverse = lax.rsqrt(jnp.mean(out * out, axis=-1, keepdims=True) + EPSILON)
    return out * inverse * gain


def renormalize(previous, grad):
    moved = previous + grad
    return moved * (
        jnp.sqrt(jnp.mean(previous * previous, axis=-1, keepdims=True) + EPSILON)
        / jnp.sqrt(jnp.mean(moved * moved, axis=-1, keepdims=True) + EPSILON)
    )


def fused_kernel(
    n, slices, q_hbm, k_hbm, v_hbm, fq_hbm, fk_hbm, fv_hbm, w_hbm, rate_ref, gain_ref, own_ref,
    mixed_ref, final_ref,
    q_ref, k_ref, v_ref, fq_ref, fk_ref, fv_ref, w_ref, hk_ref, hv_ref, att_ref, wbf_ref, acc_ref,
    land, exs, exr, chs, gsh, fin,
    load_sem, halo_send, halo_recv, ex_send, ex_recv, chain_send, chain_recv, part_send, part_recv,
    gsh_send, gsh_recv, fin_send, fin_recv, self_sem,
):
    s = lax.axis_index("seq")
    half = n // 2
    chips = half
    block_chips = chips // 2
    chip = s // 2
    core = lax.rem(s, 2)
    rows_all = q_ref.shape[0]
    heads = q_ref.shape[1] // AH
    share = final_ref.shape[1]
    sps = half // slices
    part = sps * share
    tile = WINDOW // 2

    def remote(src, dst, send, recv, target):
        return pltpu.make_async_remote_copy(
            src_ref=src, dst_ref=dst, send_sem=send, recv_sem=recv,
            device_id={"seq": target}, device_id_type=pl.DeviceIdType.MESH,
        )

    pairs = [(q_hbm, q_ref), (k_hbm, k_ref), (v_hbm, v_ref), (fq_hbm, fq_ref),
             (fk_hbm, fk_ref), (fv_hbm, fv_ref), (w_hbm, w_ref)]
    loads = [pltpu.make_async_copy(a, b, load_sem.at[i]) for i, (a, b) in enumerate(pairs)]

    @pl.when(s < half)
    def _():
        for i in (6, 4, 5, 1, 2, 0, 3):
            loads[i].start()

    @pl.when(s >= half)
    def _():
        for i in (1, 2, 0, 6, 4, 5, 3):
            loads[i].start()

    barrier = pltpu.get_barrier_semaphore()
    for step in range(1, n):
        pl.semaphore_signal(
            barrier, inc=1, device_id={"seq": lax.rem(s + step, n)},
            device_id_type=pl.DeviceIdType.MESH,
        )
    pl.semaphore_wait(barrier, n - 1)

    tail = pl.ds(rows_all - WINDOW, WINDOW)
    right = lax.rem(s + 1, n)
    halos = [
        remote(k_hbm.at[tail, :], hk_ref, halo_send.at[0], halo_recv.at[0], right),
        remote(v_hbm.at[tail, :], hv_ref, halo_send.at[1], halo_recv.at[1], right),
    ]

    @pl.when(s < n - 1)
    def _():
        for copy in halos:
            copy.start()

    @pl.when(s == 0)
    def _():
        hk_ref[...] = jnp.zeros_like(hk_ref)
        hv_ref[...] = jnp.zeros_like(hv_ref)

    bias = jnp.where(s == 0, jnp.float32(NEG), jnp.float32(0.0))

    def attend_rows(base, first):
        def one_head(h, carry):
            lanes = pl.ds(pl.multiple_of(h * AH, AH), AH)

            def at(ref, halo, i):
                if first and i < 2:
                    return halo[i * tile : (i + 1) * tile, lanes]
                return ref[pl.ds(pl.multiple_of(base + (i - 2) * tile, tile), tile), lanes]

            for t in range(2):
                keys = [at(k_ref, hk_ref, t + i) for i in range(3)]
                values = [at(v_ref, hv_ref, t + i) for i in range(3)]
                biases = [bias if first and t + i < 2 else None for i in range(2)]
                here = pl.ds(pl.multiple_of(base + t * tile, tile), tile)
                att_ref[here, lanes] = attend(q_ref[here, lanes], keys, values, biases)
            return carry

        lax.fori_loop(0, heads, one_head, 0)

    def attention():
        def later(p, carry):
            attend_rows(p * WINDOW, False)
            return carry

        lax.fori_loop(1, rows_all // WINDOW, later, 0)

        @pl.when(s > 0)
        def _():
            for copy in halos:
                copy.wait_recv()

        attend_rows(0, True)

    def apply_all():
        m = WINDOW

        def one(i, carry):
            here = pl.ds(pl.multiple_of(i * m, m), m)
            out = apply_tile(wbf_ref, fq_ref[here, :], gain_ref[...])
            mixed_ref[here, :] = (att_ref[here, :] + out).astype(mixed_ref.dtype)
            return carry

        lax.fori_loop(0, rows_all // m, one, 0)

    def make_signal():
        def one(i, carry):
            here = pl.ds(pl.multiple_of(i * tile, tile), tile)
            fv_ref[here, :] = (rate_ref[here, :] * fv_ref[here, :].astype(jnp.float32)).astype(
                jnp.bfloat16
            )
            return carry

        lax.fori_loop(0, rows_all // tile, one, 0)

    def grad_slice(i):
        slot = i % 2
        rows = slice(i * 2 * part, (i + 1) * 2 * part)
        m = min(rows_all, 1024)
        for t in range(rows_all // m):
            x = fk_ref[t * m : (t + 1) * m, :]
            signal = fv_ref[t * m : (t + 1) * m, :]
            gate = mm(wbf_ref[0, rows, :], x, NT)
            up = mm(wbf_ref[1, rows, :], x, NT)
            back = mm(wbf_ref[2, rows, :], signal, NT)
            sg = sigmoid(gate)
            active = gate * sg
            hidden = (active * up).astype(jnp.bfloat16)
            up_grad = (back * active).astype(jnp.bfloat16)
            gate_grad = (back * up * (sg * (1.0 + gate * (1.0 - sg)))).astype(jnp.bfloat16)
            terms = (mm(gate_grad, x, NN), mm(up_grad, x, NN), mm(hidden, signal, NN))
            for j in range(3):
                if t == 0:
                    acc_ref[slot, j] = terms[j]
                else:
                    acc_ref[slot, j] += terms[j]

    partner = s + 1 - 2 * core

    def exchange(i):
        return remote(exs.at[i], exr.at[i], ex_send.at[i], ex_recv.at[i], partner)

    def start_exchange(i):
        for j in range(3):
            for p in range(sps):
                row = pl.ds(pl.multiple_of((1 - core) * part + p * share, 8), share)
                exs[i, j, p] = acc_ref[i % 2, j, row, :].astype(jnp.bfloat16)
        exchange(i).start()

    def chain_copy(i, src, target):
        return remote(src, land.at[i, core], chain_send.at[i], chain_recv.at[i], target)

    def own_sum(i, j, p):
        row = pl.ds(pl.multiple_of(core * part + p * share, 8), share)
        return acc_ref[i % 2, j, row, :] + exr[i, j, p].astype(jnp.float32)

    holder = half - 2

    def gsh_copy(i, p):
        t = i * sps + p
        return remote(chs.at[i, :, p], gsh, gsh_send.at[t], gsh_recv, t)

    def finish_first(i):
        exchange(i).wait_recv()

        @pl.when(chip == 0)
        def _():
            for j in range(3):
                for p in range(sps):
                    chs[i, j, p] = own_sum(i, j, p).astype(jnp.bfloat16)

        @pl.when(chip > 0)
        def _():
            chain_copy(i, chs.at[i], lax.rem(s + 2, n)).wait_recv()
            for j in range(3):
                for p in range(sps):
                    chs[i, j, p] = (
                        own_sum(i, j, p) + land[i, core, j, p].astype(jnp.float32)
                    ).astype(jnp.bfloat16)

        chain_copy(i, chs.at[i], lax.rem(s + 2, n)).start()

        @pl.when(s == holder)
        def _():
            for p in range(sps):
                if i * sps + p == holder:
                    local = pltpu.make_async_copy(chs.at[i, :, p], gsh, self_sem)
                    local.start()
                    local.wait()
                else:
                    gsh_copy(i, p).start()

    def part_copy(i):
        return remote(land.at[i, core], land.at[i, core], part_send.at[i], part_recv.at[i], partner)

    def part_arrival(i):
        other = 1 - core
        return remote(
            land.at[i, other], land.at[i, other], part_send.at[i], part_recv.at[i], partner
        )

    def forward(i):
        chain_copy(i, land.at[i, core], lax.rem(s + 2, n)).wait_recv()

        @pl.when(chip < chips - 1)
        def _():
            chain_copy(i, land.at[i, core], lax.rem(s + 2, n)).start()

        part_copy(i).start()

    def make_middle(i):
        part_arrival(i).wait_recv()
        for h in range(2):
            for j in range(3):
                for p in range(sps):
                    low = i * 2 * part + h * part + p * share
                    w_ref[j, low : low + share, :] = renormalize(
                        w_ref[j, low : low + share, :], land[i, h, j, p].astype(jnp.float32)
                    )
        for j in range(3):
            rows = slice(i * 2 * part, (i + 1) * 2 * part)
            wbf_ref[j, rows, :] = w_ref[j, rows, :].astype(jnp.bfloat16)

    def fin_copy(i, p):
        owner = core * half + i * sps + p
        slot = chip - block_chips
        return owner, remote(
            chs.at[i, :, p], fin.at[slot], fin_send.at[i * sps + p], fin_recv.at[slot], owner
        )

    def finish_second(i):
        exchange(i).wait_recv()
        for j in range(3):
            for p in range(sps):
                chs[i, j, p] = own_sum(i, j, p).astype(jnp.bfloat16)
        for p in range(sps):
            owner, copy = fin_copy(i, p)

            @pl.when(owner != s)
            def _():
                copy.start()

            @pl.when(owner == s)
            def _():
                local = pltpu.make_async_copy(
                    chs.at[i, :, p], fin.at[chip - block_chips], self_sem
                )
                local.start()
                local.wait()

    def finals(middle):
        for b in range(block_chips):
            source = 2 * (block_chips + b) + s // half

            @pl.when(source != s)
            def _():
                remote(gsh, fin.at[b], gsh_recv, fin_recv.at[b], source).wait_recv()

        for j in range(3):
            total = fin[0, j].astype(jnp.float32)
            for b in range(1, block_chips):
                total = total + fin[b, j].astype(jnp.float32)
            final_ref[j] = renormalize(middle[j], total)

    @pl.when(s < half)
    def _():
        loads[6].wait()
        for j in range(3):
            wbf_ref[j] = w_ref[j].astype(jnp.bfloat16)
        loads[4].wait()
        loads[5].wait()
        make_signal()
        for i in range(slices):
            grad_slice(i)
            start_exchange(i)
            if i > 0:
                finish_first(i - 1)
        finish_first(slices - 1)

    for i in (1, 2, 0):
        loads[i].wait()
    attention()

    @pl.when(s >= half)
    def _():
        for i in (6, 4, 5):
            loads[i].wait()
        make_signal()
        for i in range(slices):
            forward(i)
            make_middle(i)
            grad_slice(i)
            start_exchange(i)
            if i > 0:
                finish_second(i - 1)
        finish_second(slices - 1)

    loads[3].wait()
    apply_all()

    @pl.when(s < half)
    def _():
        @pl.when(s != holder)
        def _():
            remote(gsh, gsh, gsh_send.at[0], gsh_recv, holder).wait_recv()

        finals([renormalize(own_ref[j], gsh[j].astype(jnp.float32)) for j in range(3)])
        for i in range(slices):
            chain_copy(i, chs.at[i], lax.rem(s + 2, n)).wait_send()

            @pl.when(s == holder)
            def _():
                for p in range(sps):
                    if i * sps + p != holder:
                        gsh_copy(i, p).wait_send()

    @pl.when(s >= half)
    def _():
        mine = s - half
        finals(
            [
                renormalize(
                    own_ref[j],
                    land[mine // sps, 1, j, lax.rem(mine, sps)].astype(jnp.float32),
                )
                for j in range(3)
            ]
        )
        for i in range(slices):
            @pl.when(chip < chips - 1)
            def _():
                chain_copy(i, land.at[i, core], lax.rem(s + 2, n)).wait_send()

            part_copy(i).wait_send()
            for p in range(sps):
                owner, copy = fin_copy(i, p)

                @pl.when(owner != s)
                def _():
                    copy.wait_send()

    for i in range(slices):
        exchange(i).wait_send()

    @pl.when(s < n - 1)
    def _():
        for copy in halos:
            copy.wait_send()


def shards(
    attn_query, attn_key, attn_value, fast_query, fast_key, fast_value, rates, fast_weights, gain
):
    n = lax.axis_size("seq")
    half = n // 2
    slices = min(half, SLICES)
    rows, d = fast_key.shape
    f = fast_weights.shape[1]
    share = f // n
    sps = half // slices
    part = sps * share
    initial = fast_weights[0]
    ordered = initial.reshape(2, slices, part, 3, d).transpose(3, 1, 0, 2, 4).reshape(3, f, d)
    own = lax.dynamic_slice_in_dim(initial, lax.axis_index("seq") * share, share, 0)
    own = jnp.swapaxes(own, 0, 1)
    bf = jnp.bfloat16
    vm, dma = pltpu.VMEM, pltpu.SemaphoreType.DMA
    anywhere = pl.BlockSpec(memory_space=pl.ANY)
    inside = pl.BlockSpec(memory_space=pltpu.VMEM)
    block_chips = half // 2
    mixed, final = pl.pallas_call(
        functools.partial(fused_kernel, n, slices),
        out_shape=(
            jax.ShapeDtypeStruct((rows, d), bf),
            jax.ShapeDtypeStruct((3, share, d), jnp.float32),
        ),
        in_specs=[anywhere] * 7 + [inside] * 3,
        out_specs=(inside, inside),
        scratch_shapes=[vm((rows, d), bf)] * 6
        + [
            vm((3, f, d), jnp.float32),
            vm((WINDOW, d), bf),
            vm((WINDOW, d), bf),
            vm((rows, d), jnp.float32),
            vm((3, f, d), bf),
            vm((2, 3, 2 * part, d), jnp.float32),
            vm((slices, 2, 3, sps, share, d), bf),
            vm((slices, 3, sps, share, d), bf),
            vm((slices, 3, sps, share, d), bf),
            vm((slices, 3, sps, share, d), bf),
            vm((3, share, d), bf),
            vm((block_chips, 3, share, d), bf),
            dma((7,)),
            dma((2,)),
            dma((2,)),
        ]
        + [dma((slices,))] * 6
        + [dma((half,)), dma, dma((half,)), dma((block_chips,)), dma],
        compiler_params=pltpu.CompilerParams(
            collective_id=0, has_side_effects=True, vmem_limit_bytes=LIMIT
        ),
    )(attn_query, attn_key, attn_value, fast_query, fast_key, fast_value, ordered, rates, gain, own)
    return (mixed, jnp.swapaxes(final, 0, 1)[None])


def solution(mesh):
    tokens = P("seq", "head")
    in_specs = (tokens,) * 7 + (P("head", None, None, None), P("head", None))
    out_specs = (tokens, P("head", "seq", None, None))
    return jax.shard_map(shards, mesh=mesh, in_specs=in_specs, out_specs=out_specs, check_vma=False)
```

```python
import functools
import math

import jax
import jax.numpy as jnp
from jax import lax
from jax.experimental import pallas as pl
from jax.experimental.pallas import tpu as pltpu
from jax.sharding import PartitionSpec as P

AH = 128
WINDOW = 512
EPSILON = 1e-06
NEG = -1e30
NT = (((1,), (1,)), ((), ()))
NN = (((1,), (0,)), ((), ()))
LIMIT = 60 * 1024 * 1024
SLICES = 4


def mm(a, b, dims):
    return lax.dot_general(a, b, dims, preferred_element_type=jnp.float32)


def sigmoid(v):
    return 0.5 * jnp.tanh(0.5 * v) + 0.5


def attend(q, keys, values, biases):
    rows = q.shape[0]
    factor = math.log2(math.e) / math.sqrt(AH)
    old, mid, new = (mm(q, k, NT) for k in keys)
    if biases[0] is not None:
        old = old + biases[0]
    if biases[1] is not None:
        mid = mid + biases[1]
    row = lax.broadcasted_iota(jnp.int32, (rows, rows), 0)
    col = lax.broadcasted_iota(jnp.int32, (rows, rows), 1)
    causal = col <= row
    edge = jnp.where(causal, new, old)
    top = jnp.maximum(jnp.max(edge, -1, keepdims=True), jnp.max(mid, -1, keepdims=True))
    edge = jnp.exp2((edge - top) * factor)
    mid = jnp.exp2((mid - top) * factor)
    total = jnp.sum(edge, -1, keepdims=True) + jnp.sum(mid, -1, keepdims=True)
    p_new = jnp.where(causal, edge, 0.0).astype(jnp.bfloat16)
    p_old = jnp.where(causal, 0.0, edge).astype(jnp.bfloat16)
    out = mm(p_new, values[2], NN) + mm(p_old, values[0], NN)
    out = out + mm(mid.astype(jnp.bfloat16), values[1], NN)
    return out * (1.0 / total)


def apply_tile(w_ref, x, gain):
    gate = mm(x, w_ref[0], NT)
    up = mm(x, w_ref[1], NT)
    hidden = (gate * sigmoid(gate) * up).astype(jnp.bfloat16)
    out = mm(hidden, w_ref[2], NN)
    inverse = lax.rsqrt(jnp.mean(out * out, axis=-1, keepdims=True) + EPSILON)
    return out * inverse * gain


def renormalize(previous, grad):
    moved = previous + grad
    return moved * (
        jnp.sqrt(jnp.mean(previous * previous, axis=-1, keepdims=True) + EPSILON)
        / jnp.sqrt(jnp.mean(moved * moved, axis=-1, keepdims=True) + EPSILON)
    )


def fused_kernel(
    n, slices, q_hbm, k_hbm, v_hbm, fq_hbm, fk_hbm, fv_hbm, w_hbm, rate_ref, gain_ref,
    mixed_ref, final_ref,
    q_ref, k_ref, v_ref, fq_ref, fk_ref, fv_ref, w_ref, hk_ref, hv_ref, att_ref, wbf_ref, acc_ref,
    land, exs, exr, chs, gsh, fin, own_ref,
    load_sem, own_sem, halo_send, halo_recv, ex_send, ex_recv, chain_send, chain_recv, part_send, part_recv,
    gsh_send, gsh_recv, fin_send, fin_recv, self_sem,
):
    s = lax.axis_index("seq")
    half = n // 2
    chips = half
    block_chips = chips // 2
    chip = s // 2
    core = lax.rem(s, 2)
    rows_all = q_ref.shape[0]
    heads = q_ref.shape[1] // AH
    share = final_ref.shape[1]
    sps = half // slices
    part = sps * share
    tile = WINDOW // 2

    def remote(src, dst, send, recv, target):
        return pltpu.make_async_remote_copy(
            src_ref=src, dst_ref=dst, send_sem=send, recv_sem=recv,
            device_id={"seq": target}, device_id_type=pl.DeviceIdType.MESH,
        )

    pairs = [(q_hbm, q_ref), (k_hbm, k_ref), (v_hbm, v_ref), (fq_hbm, fq_ref),
             (fk_hbm, fk_ref), (fv_hbm, fv_ref)]
    loads = [pltpu.make_async_copy(a, b, load_sem.at[i]) for i, (a, b) in enumerate(pairs)]
    weights = [
        pltpu.make_async_copy(
            w_hbm.at[:, pl.ds((h * slices + i) * part, part), :],
            w_ref.at[:, pl.ds((i * 2 + h) * part, part), :],
            load_sem.at[6 + i * 2 + h],
        )
        for i in range(slices)
        for h in range(2)
    ]
    own = pltpu.make_async_copy(
        w_hbm.at[:, pl.ds(pl.multiple_of(s * share, 8), share), :], own_ref, own_sem
    )

    @pl.when(s < half)
    def _():
        for copy in weights:
            copy.start()
        for i in (4, 5, 1, 2, 0, 3):
            loads[i].start()
        own.start()

    @pl.when(s >= half)
    def _():
        for i in (1, 2, 0):
            loads[i].start()
        for copy in weights:
            copy.start()
        for i in (4, 5, 3):
            loads[i].start()
        own.start()

    barrier = pltpu.get_barrier_semaphore()
    for step in range(1, n):
        pl.semaphore_signal(
            barrier, inc=1, device_id={"seq": lax.rem(s + step, n)},
            device_id_type=pl.DeviceIdType.MESH,
        )
    pl.semaphore_wait(barrier, n - 1)

    tail = pl.ds(rows_all - WINDOW, WINDOW)
    right = lax.rem(s + 1, n)
    halos = [
        remote(k_hbm.at[tail, :], hk_ref, halo_send.at[0], halo_recv.at[0], right),
        remote(v_hbm.at[tail, :], hv_ref, halo_send.at[1], halo_recv.at[1], right),
    ]

    @pl.when(s < n - 1)
    def _():
        for copy in halos:
            copy.start()

    @pl.when(s == 0)
    def _():
        hk_ref[...] = jnp.zeros_like(hk_ref)
        hv_ref[...] = jnp.zeros_like(hv_ref)

    bias = jnp.where(s == 0, jnp.float32(NEG), jnp.float32(0.0))

    def attend_rows(base, first):
        def one_head(h, carry):
            lanes = pl.ds(pl.multiple_of(h * AH, AH), AH)

            def at(ref, halo, i):
                if first and i < 2:
                    return halo[i * tile : (i + 1) * tile, lanes]
                return ref[pl.ds(pl.multiple_of(base + (i - 2) * tile, tile), tile), lanes]

            for t in range(2):
                keys = [at(k_ref, hk_ref, t + i) for i in range(3)]
                values = [at(v_ref, hv_ref, t + i) for i in range(3)]
                biases = [bias if first and t + i < 2 else None for i in range(2)]
                here = pl.ds(pl.multiple_of(base + t * tile, tile), tile)
                att_ref[here, lanes] = attend(q_ref[here, lanes], keys, values, biases)
            return carry

        lax.fori_loop(0, heads, one_head, 0)

    def attention():
        def later(p, carry):
            attend_rows(p * WINDOW, False)
            return carry

        lax.fori_loop(1, rows_all // WINDOW, later, 0)

        @pl.when(s > 0)
        def _():
            for copy in halos:
                copy.wait_recv()

        attend_rows(0, True)

    def apply_all():
        m = WINDOW

        def one(i, carry):
            here = pl.ds(pl.multiple_of(i * m, m), m)
            out = apply_tile(wbf_ref, fq_ref[here, :], gain_ref[...])
            mixed_ref[here, :] = (att_ref[here, :] + out).astype(mixed_ref.dtype)
            return carry

        lax.fori_loop(0, rows_all // m, one, 0)

    def grad_slice(i):
        slot = i % 2
        rows = slice(i * 2 * part, (i + 1) * 2 * part)
        m = min(rows_all, 1024)
        acc_ref[slot] = jnp.zeros_like(acc_ref[slot])

        def one(t, carry):
            here = pl.ds(pl.multiple_of(t * m, m), m)
            x = fk_ref[here, :]
            val = fv_ref[here, :]
            rate = rate_ref[:, here]
            gate = mm(wbf_ref[0, rows, :], x, NT)
            up = mm(wbf_ref[1, rows, :], x, NT)
            back = mm(wbf_ref[2, rows, :], val, NT) * rate
            sg = sigmoid(gate)
            active = gate * sg
            hidden = (active * up * rate).astype(jnp.bfloat16)
            up_grad = (back * active).astype(jnp.bfloat16)
            gate_grad = (back * up * (sg * (1.0 + gate * (1.0 - sg)))).astype(jnp.bfloat16)
            acc_ref[slot, 0] += mm(gate_grad, x, NN)
            acc_ref[slot, 1] += mm(up_grad, x, NN)
            acc_ref[slot, 2] += mm(hidden, val, NN)
            return carry

        lax.fori_loop(0, rows_all // m, one, 0)

    partner = s + 1 - 2 * core

    def exchange(i):
        return remote(exs.at[i], exr.at[i], ex_send.at[i], ex_recv.at[i], partner)

    def start_exchange(i):
        for j in range(3):
            for p in range(sps):
                row = pl.ds(pl.multiple_of((1 - core) * part + p * share, 8), share)
                exs[i, j, p] = acc_ref[i % 2, j, row, :].astype(jnp.bfloat16)
        exchange(i).start()

    ahead = lax.rem(s + 2, n)

    def chain_copy(i, j, src):
        at = i * 3 + j
        return remote(src, land.at[i, core, j], chain_send.at[at], chain_recv.at[at], ahead)

    def own_sum(i, j, p):
        row = pl.ds(pl.multiple_of(core * part + p * share, 8), share)
        return acc_ref[i % 2, j, row, :] + exr[i, j, p].astype(jnp.float32)

    holder = half - 2

    def gsh_copy(i, p):
        t = i * sps + p
        return remote(chs.at[i, :, p], gsh, gsh_send.at[t], gsh_recv, t)

    def finish_first(i):
        exchange(i).wait_recv()

        for j in range(3):
            @pl.when(chip == 0)
            def _():
                for p in range(sps):
                    chs[i, j, p] = own_sum(i, j, p).astype(jnp.bfloat16)

            @pl.when(chip > 0)
            def _():
                chain_copy(i, j, chs.at[i, j]).wait_recv()
                for p in range(sps):
                    chs[i, j, p] = (
                        own_sum(i, j, p) + land[i, core, j, p].astype(jnp.float32)
                    ).astype(jnp.bfloat16)

            chain_copy(i, j, chs.at[i, j]).start()

        @pl.when(s == holder)
        def _():
            for p in range(sps):
                if i * sps + p == holder:
                    local = pltpu.make_async_copy(chs.at[i, :, p], gsh, self_sem)
                    local.start()
                    local.wait()
                else:
                    gsh_copy(i, p).start()

    def part_copy(i, j, side):
        at = i * 3 + j
        return remote(
            land.at[i, side, j], land.at[i, side, j], part_send.at[at], part_recv.at[at], partner
        )

    def forward(i):
        for j in range(3):
            chain_copy(i, j, land.at[i, core, j]).wait_recv()

            @pl.when(chip < chips - 1)
            def _():
                chain_copy(i, j, land.at[i, core, j]).start()

            part_copy(i, j, core).start()

    def make_middle(i):
        for j in range(3):
            part_copy(i, j, 1 - core).wait_recv()
            for h in range(2):
                for p in range(sps):
                    low = i * 2 * part + h * part + p * share
                    w_ref[j, low : low + share, :] = renormalize(
                        w_ref[j, low : low + share, :], land[i, h, j, p].astype(jnp.float32)
                    )
            rows = slice(i * 2 * part, (i + 1) * 2 * part)
            wbf_ref[j, rows, :] = w_ref[j, rows, :].astype(jnp.bfloat16)

    def fin_copy(i, p):
        owner = core * half + i * sps + p
        slot = chip - block_chips
        return owner, remote(
            chs.at[i, :, p], fin.at[slot], fin_send.at[i * sps + p], fin_recv.at[slot], owner
        )

    def finish_second(i):
        exchange(i).wait_recv()
        for j in range(3):
            for p in range(sps):
                chs[i, j, p] = own_sum(i, j, p).astype(jnp.bfloat16)
        for p in range(sps):
            owner, copy = fin_copy(i, p)

            @pl.when(owner != s)
            def _():
                copy.start()

            @pl.when(owner == s)
            def _():
                local = pltpu.make_async_copy(
                    chs.at[i, :, p], fin.at[chip - block_chips], self_sem
                )
                local.start()
                local.wait()

    def finals(middle):
        for b in range(block_chips):
            source = 2 * (block_chips + b) + s // half

            @pl.when(source != s)
            def _():
                remote(gsh, fin.at[b], gsh_recv, fin_recv.at[b], source).wait_recv()

        for j in range(3):
            total = fin[0, j].astype(jnp.float32)
            for b in range(1, block_chips):
                total = total + fin[b, j].astype(jnp.float32)
            final_ref[j] = renormalize(middle[j], total)

    @pl.when(s < half)
    def _():
        for copy in weights:
            copy.wait()
        for j in range(3):
            wbf_ref[j] = w_ref[j].astype(jnp.bfloat16)
        loads[4].wait()
        loads[5].wait()
        for i in range(slices):
            grad_slice(i)
            start_exchange(i)
            finish_first(i)

    for i in (1, 2, 0):
        loads[i].wait()
    attention()

    @pl.when(s >= half)
    def _():
        for copy in weights:
            copy.wait()
        for i in (4, 5):
            loads[i].wait()
        for i in range(slices):
            forward(i)
            make_middle(i)
            grad_slice(i)
            start_exchange(i)
            if i > 0:
                finish_second(i - 1)
        finish_second(slices - 1)

    loads[3].wait()
    own.wait()
    apply_all()

    @pl.when(s < half)
    def _():
        @pl.when(s != holder)
        def _():
            remote(gsh, gsh, gsh_send.at[0], gsh_recv, holder).wait_recv()

        finals([renormalize(own_ref[j], gsh[j].astype(jnp.float32)) for j in range(3)])
        for i in range(slices):
            for j in range(3):
                chain_copy(i, j, chs.at[i, j]).wait_send()

            @pl.when(s == holder)
            def _():
                for p in range(sps):
                    if i * sps + p != holder:
                        gsh_copy(i, p).wait_send()

    @pl.when(s >= half)
    def _():
        mine = s - half
        finals(
            [
                renormalize(
                    own_ref[j],
                    land[mine // sps, 1, j, lax.rem(mine, sps)].astype(jnp.float32),
                )
                for j in range(3)
            ]
        )
        for i in range(slices):
            @pl.when(chip < chips - 1)
            def _():
                for j in range(3):
                    chain_copy(i, j, land.at[i, core, j]).wait_send()

            for j in range(3):
                part_copy(i, j, core).wait_send()
            for p in range(sps):
                owner, copy = fin_copy(i, p)

                @pl.when(owner != s)
                def _():
                    copy.wait_send()

    for i in range(slices):
        exchange(i).wait_send()

    @pl.when(s < n - 1)
    def _():
        for copy in halos:
            copy.wait_send()


def shards(
    attn_query, attn_key, attn_value, fast_query, fast_key, fast_value, rates, fast_weights, gain
):
    n = lax.axis_size("seq")
    half = n // 2
    slices = min(half, SLICES)
    rows, d = fast_key.shape
    f = fast_weights.shape[1]
    share = f // n
    sps = half // slices
    part = sps * share
    weights = jnp.swapaxes(fast_weights[0], 0, 1)
    bf = jnp.bfloat16
    vm, dma = pltpu.VMEM, pltpu.SemaphoreType.DMA
    anywhere = pl.BlockSpec(memory_space=pl.ANY)
    inside = pl.BlockSpec(memory_space=pltpu.VMEM)
    block_chips = half // 2
    mixed, final = pl.pallas_call(
        functools.partial(fused_kernel, n, slices),
        out_shape=(
            jax.ShapeDtypeStruct((rows, d), bf),
            jax.ShapeDtypeStruct((3, share, d), jnp.float32),
        ),
        in_specs=[anywhere] * 7 + [inside] * 2,
        out_specs=(inside, inside),
        scratch_shapes=[vm((rows, d), bf)] * 6
        + [
            vm((3, f, d), jnp.float32),
            vm((WINDOW, d), bf),
            vm((WINDOW, d), bf),
            vm((rows, d), jnp.float32),
            vm((3, f, d), bf),
            vm((2, 3, 2 * part, d), jnp.float32),
            vm((slices, 2, 3, sps, share, d), bf),
            vm((slices, 3, sps, share, d), bf),
            vm((slices, 3, sps, share, d), bf),
            vm((slices, 3, sps, share, d), bf),
            vm((3, share, d), bf),
            vm((block_chips, 3, share, d), bf),
            vm((3, share, d), jnp.float32),
            dma((6 + 2 * slices,)),
            dma,
            dma((2,)),
            dma((2,)),
        ]
        + [dma((slices,))] * 2
        + [dma((3 * slices,))] * 4
        + [dma((half,)), dma, dma((half,)), dma((block_chips,)), dma],
        compiler_params=pltpu.CompilerParams(
            collective_id=0, has_side_effects=True, vmem_limit_bytes=LIMIT
        ),
    )(attn_query, attn_key, attn_value, fast_query, fast_key, fast_value, weights, rates.reshape(1, rows), gain)
    return (mixed, jnp.swapaxes(final, 0, 1)[None])


def solution(mesh):
    tokens = P("seq", "head")
    in_specs = (tokens,) * 7 + (P("head", None, None, None), P("head", None))
    out_specs = (tokens, P("head", "seq", None, None))
    return jax.shard_map(shards, mesh=mesh, in_specs=in_specs, out_specs=out_specs, check_vma=False)
```
